128 devices in a mesh: space: 16 (over z, y_hi, core), tm: 8 (over y_lo, x).
Axes of the slice: x: 4, y: 4 (y_hi: 2, y_lo: 2; y = y_hi * 2 + y_lo), z: 4, core: 2. Of those that a mesh axis runs over, the one named last changes fastest.
Arguments:
- series: bfloat16 [32, 16384, 1024], P(None, 'space', 'tm'), may hold values from -1000 to 1000, as said below
Outputs:
- cross: float32 [512, 2048], P(('space', 'tm'))
The draws below stay inside these ranges and needn't reach their ends.
Inputs may be any that keep to these rules, and one draw needn't show every extreme that they name: `series`: finite pressure samples.
All inputs are finite; a program needn't handle non-finite values.
Results may differ from the reference program's by a relative error of at most 0.0003.
Values may be sent and summed in bfloat16 or wider, within the bound.
A program may use at most 192 MiB of HBM per device.

```python
import math
import jax
import jax.numpy as jnp
from jax import lax

M = 32
NT = 1024
NPTS = 16384


def draw_series(key, part):
    key_modes = jax.random.fold_in(key, 11)
    key_coeffs = jax.random.fold_in(key, 12)
    key_offset = jax.random.fold_in(key, 13)
    key_noise = jax.random.fold_in(key, 14)
    amplitude = [2.0, 1.5, 1.1, 0.8]
    modes = jax.random.normal(key_modes, (4, NPTS), jnp.float32)
    coeffs = jax.random.normal(key_coeffs, (M, 4, NT), jnp.float32)
    offset = 2.0 * jax.random.normal(key_offset, (NPTS,), jnp.float32)
    noise = jax.random.normal(key_noise, (M, NPTS, NT), jnp.float32)
    total = 0.8 * noise
    for index in range(4):
        total = total + amplitude[index] * coeffs[:, index, None, :] * modes[index][None, :, None]
    total = total + offset[None, :, None]
    return total.astype(jnp.bfloat16)


def setup_inputs(seed: int = 0) -> dict:
    splits = jax.random.split(jax.random.key(seed), 2)
    series = draw_series(jax.random.fold_in(splits[1], 71), 0)
    return {"series": series}


def reference(series):
    members, points, frames = series.shape
    nfreq = frames // 2
    time_index = jnp.arange(frames, dtype=jnp.float32)
    window = 0.5 - 0.5 * jnp.cos(2.0 * math.pi * time_index / frames)
    width = math.gcd(points, 256)
    count = points // width
    norm_factor = 1.0 / (0.375 * frames * points)

    def accumulate(running, index):
        first_point = (index * width).astype(jnp.int32)
        segment = lax.dynamic_slice_in_dim(series, first_point, width, 1).astype(jnp.float32)
        time_mean = jnp.mean(segment, axis=2, keepdims=True)
        fluctuation = (segment - time_mean) * window
        transform = jnp.fft.rfft(fluctuation, axis=2)[:, :, :nfreq]
        real_part = jnp.real(transform).astype(jnp.float32)
        imag_part = jnp.imag(transform).astype(jnp.float32)
        shaped = jnp.stack([real_part, imag_part], axis=2)
        gram_all = jnp.einsum("ipcf,jpdf->fcdij", shaped, shaped, precision=lax.Precision.HIGHEST)
        return running + gram_all, None

    running = jnp.zeros((nfreq, 2, 2, members, members), jnp.float32)
    running, _ = lax.scan(accumulate, running, jnp.arange(count, dtype=jnp.int32))
    real_sum = running[:, 0, 0] + running[:, 1, 1]
    imag_sum = running[:, 1, 0] - running[:, 0, 1]
    return (jnp.stack([real_sum, imag_sum], axis=1).reshape(nfreq, 2 * members * members) * norm_factor).astype(jnp.float32)
```

```python
import functools
import math

import jax
import jax.numpy as jnp
import ml_dtypes
import numpy as np
from jax import lax
from jax.experimental import pallas as pl
from jax.experimental.pallas import tpu as pltpu
from jax.sharding import PartitionSpec as P

MESH = pl.DeviceIdType.MESH
NT_DIMS = (((1,), (1,)), ((), ()))
CHUNKS = 8
FBLOCK = 128
TM_PEERS = ((1, 0), (2, 1), (3, 0), (0, 1), (1, 1), (2, 0), (3, 1))


def dft_table(frames):
    nfreq = frames // 2
    t = np.arange(frames)
    angle = 2.0 * np.pi * (np.arange(nfreq)[:, None] * t[None, :] % frames) / frames
    window = 0.5 - 0.5 * np.cos(2.0 * np.pi * t / frames)
    table = np.stack([np.cos(angle), -np.sin(angle)]) * window
    table = table - table.sum(axis=2, keepdims=True) / frames
    table[np.abs(table) < 1e-13] = 0.0
    bf16 = ml_dtypes.bfloat16
    high = table.astype(np.float32).astype(bf16)
    low = (table - high.astype(np.float64)).astype(np.float32).astype(bf16)
    high = high.reshape(2 * nfreq, frames)
    low = low.reshape(2 * nfreq, frames)
    order = np.argsort(np.abs(low.astype(np.float64)), axis=1)
    for first, count in ((0, 32), (32, 4), (36, 1), (37, 1)):
        rest = (high.astype(np.float64) + low.astype(np.float64)).sum(axis=1, keepdims=True)
        cols = order[:, first : first + count]
        rows = np.arange(2 * nfreq)[:, None]
        low[rows, cols] = (low[rows, cols].astype(np.float64) - rest / count).astype(np.float32).astype(bf16)
    parts = np.stack([high, low]).reshape(2, 2, nfreq // FBLOCK, FBLOCK, frames)
    return parts.transpose(2, 0, 1, 3, 4).reshape(nfreq // FBLOCK, 2, 2 * FBLOCK, frames)


def split(value):
    high = value.astype(jnp.bfloat16)
    return high, (value - high.astype(jnp.float32)).astype(jnp.bfloat16)


def matmul_nt(a, b):
    return lax.dot_general(a, b, NT_DIMS, preferred_element_type=jnp.float32)


def kernel(
    norm, x_ref, table_ref, o_ref,
    recv, table, xre, xim, part_z, part_p, core_z, core_p, got_z, got_zp, got_p, got_pz,
    local_sem, table_sem, a2a_send, a2a_recv, core_send, core_recv, z_send, z_recv, p_send, p_recv,
):
    space, tm = lax.axis_index("space"), lax.axis_index("tm")
    core, y_hi, z = space % 2, space // 2 % 2, space // 4
    x, y_lo = tm % 4, tm // 4
    members, block = recv.shape[1], recv.shape[2]
    per_chunk = members // CHUNKS
    nfreq = xre.shape[0] // members
    plane = y_hi * 8 + y_lo * 4 + x

    def tm_peer(r):
        dx, dy = TM_PEERS[r]
        return (y_lo + dy) % 2 * 4 + (x + dx) % 4

    def tm_source(r):
        dx, dy = TM_PEERS[r]
        return (y_lo + 2 - dy) % 2 * 4 + (x + 4 - dx) % 4

    def device(z, plane, core):
        return z * 4 + plane // 8 * 2 + core, plane % 8

    def plane_peer(d):
        dyh, dyl, dx = d // 8, d // 4 % 2, d % 4
        ahead = (y_hi + dyh) % 2 * 8 + (y_lo + dyl) % 2 * 4 + (x + dx) % 4
        return ahead

    barrier = pltpu.get_barrier_semaphore()
    greeted = [device(z, plane_peer(d), core) for d in range(1, 16)]
    greeted += [device((z + d) % 4, plane, core) for d in range(1, 4)]
    greeted += [device(z, plane, 1 - core)]
    for peer in greeted:
        pl.semaphore_signal(barrier, inc=1, device_id=peer, device_id_type=MESH)
    pl.semaphore_wait(barrier, len(greeted))

    def snapshots(c, r):
        peer = tm_peer(r)
        return pltpu.make_async_remote_copy(
            src_ref=x_ref.at[pl.ds(c * per_chunk, per_chunk), pl.ds(peer * block, block), :],
            dst_ref=recv.at[tm, pl.ds(c * per_chunk, per_chunk)],
            send_sem=a2a_send.at[c, r],
            recv_sem=a2a_recv.at[c, r],
            device_id=(space, peer),
            device_id_type=MESH,
        )

    @pl.loop(0, CHUNKS)
    def _(c):
        for r in range(len(TM_PEERS)):
            snapshots(c, r).start()

    table_copy = pltpu.make_async_copy(table_ref, table, table_sem)
    table_copy.start()
    own_copy = pltpu.make_async_copy(x_ref.at[:, pl.ds(tm * block, block), :], recv.at[tm], local_sem)
    own_copy.start()
    table_copy.wait()
    own_copy.wait()

    @pl.loop(0, CHUNKS)
    def _(c):
        for r in range(len(TM_PEERS)):
            snapshots(c, r).wait_recv()
        first = c * per_chunk

        @pl.loop(0, nfreq // FBLOCK)
        def _(b):
            samples = jnp.concatenate(
                [recv[k, pl.ds(first, per_chunk)].reshape(per_chunk * block, block) for k in range(8)], axis=1
            )
            spectra = matmul_nt(table[b, 0], samples) + matmul_nt(table[b, 1], samples)
            for m in range(per_chunk):
                rows = pl.ds(b * (FBLOCK * members) + first + m, FBLOCK, stride=members)
                columns = slice(m * block, (m + 1) * block)
                xre[rows, :] = spectra[:FBLOCK, columns]
                xim[rows, :] = spectra[FBLOCK:, columns]

    lane = lax.broadcasted_iota(jnp.int32, (members, 4 * members), 1)
    row = lax.broadcasted_iota(jnp.int32, (members, 4 * members), 0)
    lane_f, lane_j = lane // members, lane % members
    half = members // 2

    def pick(tile):
        out = tile[3 * members :]
        for f in range(3):
            out = jnp.where(lane_f == f, tile[f * members : (f + 1) * members], out)
        return out

    def cross(zz, pp, cc):
        sp, t = device(zz, pp, cc)
        rows = pl.ds((sp * 8 + t) * (4 * members), 4 * members)
        re_hi, re_lo = split(xre[rows, :])
        im_hi, im_lo = split(xim[rows, :])
        a_hi = jnp.concatenate([re_hi, im_hi], axis=1)
        a_lo = jnp.concatenate([re_lo, im_lo], axis=1)
        b_hi = jnp.concatenate([a_hi, jnp.concatenate([-im_hi, re_hi], axis=1)], axis=0)
        b_lo = jnp.concatenate([a_lo, jnp.concatenate([-im_lo, re_lo], axis=1)], axis=0)
        gram = matmul_nt(a_hi, b_hi) + matmul_nt(a_lo, b_hi) + matmul_nt(a_hi, b_lo)
        return jnp.where(row >= lane_j, pick(gram[:, : 4 * members]), pick(gram[:, 4 * members :]))

    other = 1 - core

    @pl.loop(0, 64)
    def _(n):
        zz, pp = n // 16, n % 16
        tile = cross(zz, pp, other)
        part_z[0, zz, pp] = tile[:half]
        part_p[0, pp, zz] = tile[half:]

    def to_core(k):
        return pltpu.make_async_remote_copy(
            src_ref=(part_z, part_p)[k].at[0],
            dst_ref=(core_z, core_p)[k],
            send_sem=core_send.at[k],
            recv_sem=core_recv.at[k],
            device_id=(space + 1 - 2 * core, tm),
            device_id_type=MESH,
        )

    for k in range(2):
        to_core(k).start()

    @pl.loop(0, 64)
    def _(n):
        zz, pp = n // 16, n % 16
        tile = cross(zz, pp, core)
        part_z[1, zz, pp] = tile[:half]
        part_p[1, pp, zz] = tile[half:]

    for k in range(2):
        to_core(k).wait_recv()
    part_z[1] += core_z[...]
    part_p[1] += core_p[...]

    def over_z(stage, d):
        zz = (z + d) % 4
        src, dst = ((part_z.at[1, zz], got_z.at[d]), (part_p.at[1, plane, zz], got_pz.at[d]))[stage]
        return pltpu.make_async_remote_copy(
            src_ref=src,
            dst_ref=dst,
            send_sem=z_send.at[stage, d],
            recv_sem=z_recv.at[stage, d],
            device_id=device(zz, plane, core),
            device_id_type=MESH,
        )

    def over_plane(stage, d):
        pp = plane_peer(d)
        src, dst = ((part_p.at[1, pp], got_p.at[d]), (part_z.at[1, z, pp], got_zp.at[d]))[stage]
        return pltpu.make_async_remote_copy(
            src_ref=src,
            dst_ref=dst,
            send_sem=p_send.at[stage, d],
            recv_sem=p_recv.at[stage, d],
            device_id=device(z, pp, core),
            device_id_type=MESH,
        )

    for d in range(1, 4):
        over_z(0, d).start()
    for d in range(1, 16):
        over_plane(0, d).start()
    for d in range(1, 4):
        over_z(0, d).wait_recv()
    total = part_z[1, z]
    for d in range(1, 4):
        total = total + got_z[d]
    part_z[1, z] = total
    for d in range(1, 16):
        over_plane(1, d).start()
    for d in range(1, 16):
        over_plane(0, d).wait_recv()
    total = part_p[1, plane]
    for d in range(1, 16):
        total = total + got_p[d]
    part_p[1, plane] = total
    for d in range(1, 4):
        over_z(1, d).start()
    for d in range(1, 16):
        over_plane(1, d).wait_recv()
    upper = part_z[1, z, plane]
    for d in range(1, 16):
        upper = upper + got_zp[d]
    for d in range(1, 4):
        over_z(1, d).wait_recv()
    lower = part_p[1, plane, z]
    for d in range(1, 4):
        lower = lower + got_pz[d]

    mixed = jnp.concatenate([upper, lower], axis=0) * norm
    spread = jnp.concatenate([jnp.where(lane_f == f, mixed, 0.0) for f in range(4)], axis=0).T
    turned = spread[:members]
    for f in range(1, 4):
        turned = turned + spread[f * members : (f + 1) * members]
    real = jnp.where(row >= lane_j, mixed, turned)
    imag = jnp.where(row < lane_j, mixed, jnp.where(row == lane_j, 0.0, -turned))
    for part, value in enumerate((real, imag)):
        for bit in (2, 1):
            row_bit, lane_bit = row // bit % 2, lane_f // bit % 2
            up = pltpu.roll(pltpu.roll(value, bit * members, 1), members - bit, 0)
            down = pltpu.roll(pltpu.roll(value, (4 - bit) * members, 1), bit, 0)
            value = jnp.where(row_bit == lane_bit, value, jnp.where(row_bit == 0, up, down))
        for u in range(members // 4):
            start = (part * members // 4 + u) * 4 * members
            o_ref[:, start : start + 4 * members] = value[4 * u : 4 * u + 4]

    @pl.loop(0, CHUNKS)
    def _(c):
        for r in range(len(TM_PEERS)):
            snapshots(c, r).wait_send()

    for k in range(2):
        to_core(k).wait_send()
    for stage in range(2):
        for d in range(1, 4):
            over_z(stage, d).wait_send()
        for d in range(1, 16):
            over_plane(stage, d).wait_send()


def shards(series):
    members, pts_dev, frames_dev = series.shape
    space_count, time_count = lax.axis_size("space"), lax.axis_size("tm")
    frames, block = frames_dev * time_count, pts_dev // time_count
    nfreq, half = frames // 2, members // 2
    norm = 1.0 / (0.375 * frames * pts_dev * space_count)
    table = dft_table(frames)
    f32, bf16 = jnp.float32, jnp.bfloat16
    width = 4 * members
    dma = pltpu.SemaphoreType.DMA
    return pl.pallas_call(
        functools.partial(kernel, norm),
        out_shape=jax.ShapeDtypeStruct((nfreq // (space_count * time_count), 2 * members * members), f32),
        in_specs=[pl.BlockSpec(memory_space=pl.ANY)] * 2,
        out_specs=pl.BlockSpec(memory_space=pltpu.VMEM),
        scratch_shapes=[
            pltpu.VMEM((time_count, members, block, frames_dev), bf16),
            pltpu.VMEM(table.shape, bf16),
            pltpu.VMEM((nfreq * members, block), f32),
            pltpu.VMEM((nfreq * members, block), f32),
            pltpu.VMEM((2, 4, 16, half, width), f32),
            pltpu.VMEM((2, 16, 4, half, width), f32),
            pltpu.VMEM((4, 16, half, width), f32),
            pltpu.VMEM((16, 4, half, width), f32),
            pltpu.VMEM((4, 16, half, width), f32),
            pltpu.VMEM((16, half, width), f32),
            pltpu.VMEM((16, 4, half, width), f32),
            pltpu.VMEM((4, half, width), f32),
            dma, dma, dma((CHUNKS, 7)), dma((CHUNKS, 7)), dma((2,)), dma((2,)),
            dma((2, 4)), dma((2, 4)), dma((2, 16)), dma((2, 16)),
        ],
        compiler_params=pltpu.CompilerParams(collective_id=0, has_side_effects=True, vmem_limit_bytes=56 << 20),
    )(series, jnp.asarray(table))


def solution(mesh):
    placed = (P(None, "space", "tm"),)
    return jax.shard_map(
        shards, mesh=mesh, in_specs=placed, out_specs=P(("space", "tm"), None), check_vma=False
    )
```

```python
import functools
import math

import jax
import jax.numpy as jnp
import ml_dtypes
import numpy as np
from jax import lax
from jax.experimental import pallas as pl
from jax.experimental.pallas import tpu as pltpu
from jax.sharding import PartitionSpec as P

MESH = pl.DeviceIdType.MESH
NT_DIMS = (((1,), (1,)), ((), ()))
CHUNKS = 8
FBLOCK = 128
TM_PEERS = ((1, 0), (2, 1), (3, 0), (0, 1), (1, 1), (2, 0), (3, 1))


def dft_table(frames):
    nfreq = frames // 2
    t = np.arange(frames)
    angle = 2.0 * np.pi * (np.arange(nfreq)[:, None] * t[None, :] % frames) / frames
    window = 0.5 - 0.5 * np.cos(2.0 * np.pi * t / frames)
    table = np.stack([np.cos(angle), -np.sin(angle)]) * window
    table = table - table.sum(axis=2, keepdims=True) / frames
    table[np.abs(table) < 1e-13] = 0.0
    bf16 = ml_dtypes.bfloat16
    high = table.astype(np.float32).astype(bf16)
    low = (table - high.astype(np.float64)).astype(np.float32).astype(bf16)
    high = high.reshape(2 * nfreq, frames)
    low = low.reshape(2 * nfreq, frames)
    order = np.argsort(np.abs(low.astype(np.float64)), axis=1)
    for first, count in ((0, 32), (32, 4), (36, 1), (37, 1)):
        rest = (high.astype(np.float64) + low.astype(np.float64)).sum(axis=1, keepdims=True)
        cols = order[:, first : first + count]
        rows = np.arange(2 * nfreq)[:, None]
        low[rows, cols] = (low[rows, cols].astype(np.float64) - rest / count).astype(np.float32).astype(bf16)
    parts = np.stack([high, low]).reshape(2, 2, nfreq // FBLOCK, FBLOCK, frames)
    return parts.transpose(2, 0, 1, 3, 4).reshape(nfreq // FBLOCK, 2, 2 * FBLOCK, frames)


def split(value):
    high = value.astype(jnp.bfloat16)
    return high, (value - high.astype(jnp.float32)).astype(jnp.bfloat16)


def matmul_nt(a, b):
    return lax.dot_general(a, b, NT_DIMS, preferred_element_type=jnp.float32)


def kernel(
    norm, x_ref, table_ref, o_ref,
    recv, table, xre, xim, part, got_core, got_z, got_zp, got_p, got_pz,
    local_sem, table_sem, a2a_send, a2a_recv, core_send, core_recv, z_send, z_recv, p_send, p_recv,
):
    space, tm = lax.axis_index("space"), lax.axis_index("tm")
    core, y_hi, z = space % 2, space // 2 % 2, space // 4
    x, y_lo = tm % 4, tm // 4
    members, block = recv.shape[1], recv.shape[2]
    per_chunk = members // CHUNKS
    nfreq = xre.shape[0] // members
    plane = y_hi * 8 + y_lo * 4 + x

    def tm_peer(r):
        dx, dy = TM_PEERS[r]
        return (y_lo + dy) % 2 * 4 + (x + dx) % 4

    def tm_source(r):
        dx, dy = TM_PEERS[r]
        return (y_lo + 2 - dy) % 2 * 4 + (x + 4 - dx) % 4

    def device(z, plane, core):
        return z * 4 + plane // 8 * 2 + core, plane % 8

    def plane_peer(d):
        dyh, dyl, dx = d // 8, d // 4 % 2, d % 4
        ahead = (y_hi + dyh) % 2 * 8 + (y_lo + dyl) % 2 * 4 + (x + dx) % 4
        return ahead

    barrier = pltpu.get_barrier_semaphore()
    greeted = [device(z, plane_peer(d), core) for d in range(1, 16)]
    greeted += [device((z + d) % 4, plane, core) for d in range(1, 4)]
    greeted += [device(z, plane, 1 - core)]
    for peer in greeted:
        pl.semaphore_signal(barrier, inc=1, device_id=peer, device_id_type=MESH)
    pl.semaphore_wait(barrier, len(greeted))

    def snapshots(c, r):
        peer = tm_peer(r)
        return pltpu.make_async_remote_copy(
            src_ref=x_ref.at[pl.ds(c * per_chunk, per_chunk), pl.ds(peer * block, block), :],
            dst_ref=recv.at[tm, pl.ds(c * per_chunk, per_chunk)],
            send_sem=a2a_send.at[c, r],
            recv_sem=a2a_recv.at[c, r],
            device_id=(space, peer),
            device_id_type=MESH,
        )

    @pl.loop(0, CHUNKS)
    def _(c):
        for r in range(len(TM_PEERS)):
            snapshots(c, r).start()

    table_copy = pltpu.make_async_copy(table_ref, table, table_sem)
    table_copy.start()
    own_copy = pltpu.make_async_copy(x_ref.at[:, pl.ds(tm * block, block), :], recv.at[tm], local_sem)
    own_copy.start()
    table_copy.wait()
    own_copy.wait()

    @pl.loop(0, CHUNKS)
    def _(c):
        for r in range(len(TM_PEERS)):
            snapshots(c, r).wait_recv()
        first = c * per_chunk

        @pl.loop(0, nfreq // FBLOCK)
        def _(b):
            samples = jnp.concatenate(
                [recv[k, pl.ds(first, per_chunk)].reshape(per_chunk * block, block) for k in range(8)], axis=1
            )
            spectra = matmul_nt(table[b, 0], samples) + matmul_nt(table[b, 1], samples)
            for m in range(per_chunk):
                rows = pl.ds(b * (FBLOCK * members) + first + m, FBLOCK, stride=members)
                columns = slice(m * block, (m + 1) * block)
                xre[rows, :] = spectra[:FBLOCK, columns]
                xim[rows, :] = spectra[FBLOCK:, columns]

    lane = lax.broadcasted_iota(jnp.int32, (members, 4 * members), 1)
    row = lax.broadcasted_iota(jnp.int32, (members, 4 * members), 0)
    lane_f, lane_j = lane // members, lane % members
    half = members // 2

    def pick(tile):
        out = tile[3 * members :]
        for f in range(3):
            out = jnp.where(lane_f == f, tile[f * members : (f + 1) * members], out)
        return out

    def cross(zz, yy, t, cc):
        width = 4 * members
        rows = pl.ds((zz * 32 + yy * 16 + cc * 8 + t) * width, width)
        re_hi, re_lo = split(xre[rows, :])
        im_hi, im_lo = split(xim[rows, :])
        a_hi = jnp.concatenate([re_hi, im_hi], axis=1)
        a_lo = jnp.concatenate([re_lo, im_lo], axis=1)
        b_hi = jnp.concatenate([a_hi, jnp.concatenate([-im_hi, re_hi], axis=1)], axis=0)
        b_lo = jnp.concatenate([a_lo, jnp.concatenate([-im_lo, re_lo], axis=1)], axis=0)
        both = matmul_nt(jnp.concatenate([a_hi, a_lo], axis=0), b_hi)
        gram = both[:width] + both[width:] + matmul_nt(a_hi, b_lo)
        return jnp.where(row >= lane_j, pick(gram[:, :width]), pick(gram[:, width:]))

    def to_core(n):
        zz = (z + 1 + n) % 4
        return pltpu.make_async_remote_copy(
            src_ref=part.at[0, zz],
            dst_ref=got_core.at[zz],
            send_sem=core_send.at[n],
            recv_sem=core_recv.at[n],
            device_id=(space + 1 - 2 * core, tm),
            device_id_type=MESH,
        )

    def over_z(stage, d):
        zz = (z + d) % 4
        src, dst = ((part.at[1, zz, 0], got_z.at[d]), (part.at[1, zz, 1, plane], got_pz.at[d]))[stage]
        return pltpu.make_async_remote_copy(
            src_ref=src,
            dst_ref=dst,
            send_sem=z_send.at[stage, d],
            recv_sem=z_recv.at[stage, d],
            device_id=device(zz, plane, core),
            device_id_type=MESH,
        )

    def over_plane(n, d):
        pp, zz = plane_peer(d), (z + 1 + n) % 4
        src, dst = (part.at[1, zz, 1, pp], got_p.at[zz, d])
        if isinstance(n, int) and n == 4:
            src, dst = part.at[1, z, 0, pp], got_zp.at[d]
        return pltpu.make_async_remote_copy(
            src_ref=src,
            dst_ref=dst,
            send_sem=p_send.at[n, d],
            recv_sem=p_recv.at[n, d],
            device_id=device(z, pp, core),
            device_id_type=MESH,
        )

    @pl.loop(0, 4)
    def _(n):
        zz = (z + 1 + n) % 4

        @pl.loop(0, 2)
        def _(yy):
            for t in range(8):
                tile = cross(zz, yy, t, 1 - core)
                part[0, zz, 0, yy * 8 + t] = tile[:half]
                part[0, zz, 1, yy * 8 + t] = tile[half:]

        to_core(n).start()

    @pl.loop(0, 4)
    def _(n):
        zz = (z + 1 + n) % 4
        to_core(n).wait_recv()

        @pl.loop(0, 2)
        def _(yy):
            for t in range(8):
                tile = cross(zz, yy, t, core)
                pp = yy * 8 + t
                part[1, zz, 0, pp] = tile[:half] + got_core[zz, 0, pp]
                part[1, zz, 1, pp] = tile[half:] + got_core[zz, 1, pp]

        @pl.when(n < 3)
        def _():
            over_z(0, n + 1).start()

        for d in range(1, 16):
            over_plane(n, d).start()

    def lower_sum(n):
        zz = (z + 1 + n) % 4
        for d in range(1, 16):
            over_plane(n, d).wait_recv()
        total = part[1, zz, 1, plane]
        for d in range(1, 16):
            total = total + got_p[zz, d]
        return total

    for n in range(3):
        part[1, (z + 1 + n) % 4, 1, plane] = lower_sum(n)
        over_z(1, n + 1).start()
    for d in range(1, 4):
        over_z(0, d).wait_recv()
    part[1, z, 0] += got_z[1] + got_z[2] + got_z[3]
    for d in range(1, 16):
        over_plane(4, d).start()
    lower = lower_sum(3)
    for d in range(1, 4):
        over_z(1, d).wait_recv()
        lower = lower + got_pz[d]
    upper = part[1, z, 0, plane]
    for d in range(1, 16):
        over_plane(4, d).wait_recv()
        upper = upper + got_zp[d]

    mixed = jnp.concatenate([upper, lower], axis=0) * norm
    spread = jnp.concatenate([jnp.where(lane_f == f, mixed, 0.0) for f in range(4)], axis=0).T
    turned = spread[:members]
    for f in range(1, 4):
        turned = turned + spread[f * members : (f + 1) * members]
    real = jnp.where(row >= lane_j, mixed, turned)
    imag = jnp.where(row < lane_j, mixed, jnp.where(row == lane_j, 0.0, -turned))
    for which, value in enumerate((real, imag)):
        for bit in (2, 1):
            row_bit, lane_bit = row // bit % 2, lane_f // bit % 2
            up = pltpu.roll(pltpu.roll(value, bit * members, 1), members - bit, 0)
            down = pltpu.roll(pltpu.roll(value, (4 - bit) * members, 1), bit, 0)
            value = jnp.where(row_bit == lane_bit, value, jnp.where(row_bit == 0, up, down))
        for u in range(members // 4):
            start = (which * members // 4 + u) * 4 * members
            o_ref[:, start : start + 4 * members] = value[4 * u : 4 * u + 4]

    @pl.loop(0, CHUNKS)
    def _(c):
        for r in range(len(TM_PEERS)):
            snapshots(c, r).wait_send()

    for n in range(4):
        to_core(n).wait_send()
    for d in range(1, 4):
        over_z(0, d).wait_send()
        over_z(1, d).wait_send()
    for n in range(5):
        for d in range(1, 16):
            over_plane(n, d).wait_send()


def shards(series):
    members, pts_dev, frames_dev = series.shape
    space_count, time_count = lax.axis_size("space"), lax.axis_size("tm")
    frames, block = frames_dev * time_count, pts_dev // time_count
    nfreq, half = frames // 2, members // 2
    norm = 1.0 / (0.375 * frames * pts_dev * space_count)
    table = dft_table(frames)
    f32, bf16 = jnp.float32, jnp.bfloat16
    width = 4 * members
    dma = pltpu.SemaphoreType.DMA
    return pl.pallas_call(
        functools.partial(kernel, norm),
        out_shape=jax.ShapeDtypeStruct((nfreq // (space_count * time_count), 2 * members * members), f32),
        in_specs=[pl.BlockSpec(memory_space=pl.ANY)] * 2,
        out_specs=pl.BlockSpec(memory_space=pltpu.VMEM),
        scratch_shapes=[
            pltpu.VMEM((time_count, members, block, frames_dev), bf16),
            pltpu.VMEM(table.shape, bf16),
            pltpu.VMEM((nfreq * members, block), f32),
            pltpu.VMEM((nfreq * members, block), f32),
            pltpu.VMEM((2, 4, 2, 16, half, width), f32),
            pltpu.VMEM((4, 2, 16, half, width), f32),
            pltpu.VMEM((4, 16, half, width), f32),
            pltpu.VMEM((16, half, width), f32),
            pltpu.VMEM((4, 16, half, width), f32),
            pltpu.VMEM((4, half, width), f32),
            dma, dma, dma((CHUNKS, 7)), dma((CHUNKS, 7)), dma((4,)), dma((4,)),
            dma((2, 4)), dma((2, 4)), dma((5, 16)), dma((5, 16)),
        ],
        compiler_params=pltpu.CompilerParams(collective_id=0, has_side_effects=True, vmem_limit_bytes=56 << 20),
    )(series, jnp.asarray(table))


def solution(mesh):
    placed = (P(None, "space", "tm"),)
    return jax.shard_map(
        shards, mesh=mesh, in_specs=placed, out_specs=P(("space", "tm"), None), check_vma=False
    )
```

```python
import functools
import math

import jax
import jax.numpy as jnp
import ml_dtypes
import numpy as np
from jax import lax
from jax.experimental import pallas as pl
from jax.experimental.pallas import tpu as pltpu
from jax.sharding import PartitionSpec as P

MESH = pl.DeviceIdType.MESH
NT_DIMS = (((1,), (1,)), ((), ()))
CHUNKS = 8
FBLOCK = 128
TM_PEERS = ((1, 0), (2, 1), (3, 0), (0, 1), (1, 1), (2, 0), (3, 1))


def dft_table(frames):
    nfreq = frames // 2
    t = np.arange(frames)
    angle = 2.0 * np.pi * (np.arange(nfreq)[:, None] * t[None, :] % frames) / frames
    window = 0.5 - 0.5 * np.cos(2.0 * np.pi * t / frames)
    table = np.stack([np.cos(angle), -np.sin(angle)]) * window
    table = table - table.sum(axis=2, keepdims=True) / frames
    table[np.abs(table) < 1e-13] = 0.0
    bf16 = ml_dtypes.bfloat16
    high = table.astype(np.float32).astype(bf16)
    low = (table - high.astype(np.float64)).astype(np.float32).astype(bf16)
    high = high.reshape(2 * nfreq, frames)
    low = low.reshape(2 * nfreq, frames)
    order = np.argsort(np.abs(low.astype(np.float64)), axis=1)
    for first, count in ((0, 32), (32, 4), (36, 1), (37, 1)):
        rest = (high.astype(np.float64) + low.astype(np.float64)).sum(axis=1, keepdims=True)
        cols = order[:, first : first + count]
        rows = np.arange(2 * nfreq)[:, None]
        low[rows, cols] = (low[rows, cols].astype(np.float64) - rest / count).astype(np.float32).astype(bf16)
    parts = np.stack([high, low]).reshape(2, 2, nfreq // FBLOCK, FBLOCK, frames)
    return parts.transpose(2, 0, 1, 3, 4).reshape(nfreq // FBLOCK, 2, 2 * FBLOCK, frames)


def split(value):
    high = value.astype(jnp.bfloat16)
    return high, (value - high.astype(jnp.float32)).astype(jnp.bfloat16)


def matmul_nt(a, b):
    return lax.dot_general(a, b, NT_DIMS, preferred_element_type=jnp.float32)


def matmul(a, b):
    return jnp.dot(a, b, preferred_element_type=jnp.float32)


def kernel(
    norm, x_ref, table_ref, o_ref,
    recv, table, xre, xim, part, got_core, got_z, got_zp, got_p, got_pz,
    local_sem, table_sem, a2a_send, a2a_recv, core_send, core_recv, z_send, z_recv, p_send, p_recv,
):
    space, tm = lax.axis_index("space"), lax.axis_index("tm")
    core, y_hi, z = space % 2, space // 2 % 2, space // 4
    x, y_lo = tm % 4, tm // 4
    members, block = recv.shape[1], recv.shape[2]
    per_chunk = members // CHUNKS
    nfreq = xre.shape[0] // members
    plane = y_hi * 8 + y_lo * 4 + x

    def tm_peer(r):
        dx, dy = TM_PEERS[r]
        return (y_lo + dy) % 2 * 4 + (x + dx) % 4

    def tm_source(r):
        dx, dy = TM_PEERS[r]
        return (y_lo + 2 - dy) % 2 * 4 + (x + 4 - dx) % 4

    def device(z, plane, core):
        return z * 4 + plane // 8 * 2 + core, plane % 8

    def plane_peer(d):
        dyh, dyl, dx = d // 8, d // 4 % 2, d % 4
        ahead = (y_hi + dyh) % 2 * 8 + (y_lo + dyl) % 2 * 4 + (x + dx) % 4
        return ahead

    barrier = pltpu.get_barrier_semaphore()
    greeted = [device(z, plane_peer(d), core) for d in range(1, 16)]
    greeted += [device((z + d) % 4, plane, core) for d in range(1, 4)]
    greeted += [device(z, plane, 1 - core)]
    for peer in greeted:
        pl.semaphore_signal(barrier, inc=1, device_id=peer, device_id_type=MESH)
    pl.semaphore_wait(barrier, len(greeted))

    def snapshots(c, r):
        peer = tm_peer(r)
        return pltpu.make_async_remote_copy(
            src_ref=x_ref.at[pl.ds(c * per_chunk, per_chunk), pl.ds(peer * block, block), :],
            dst_ref=recv.at[tm, pl.ds(c * per_chunk, per_chunk)],
            send_sem=a2a_send.at[c, r],
            recv_sem=a2a_recv.at[c, r],
            device_id=(space, peer),
            device_id_type=MESH,
        )

    @pl.loop(0, CHUNKS)
    def _(c):
        for r in range(len(TM_PEERS)):
            snapshots(c, r).start()

    table_copy = pltpu.make_async_copy(table_ref, table, table_sem)
    table_copy.start()
    own_copy = pltpu.make_async_copy(x_ref.at[:, pl.ds(tm * block, block), :], recv.at[tm], local_sem)
    own_copy.start()
    table_copy.wait()
    own_copy.wait()

    @pl.loop(0, CHUNKS)
    def _(c):
        for r in range(len(TM_PEERS)):
            snapshots(c, r).wait_recv()
        first = c * per_chunk

        @pl.loop(0, nfreq // FBLOCK)
        def _(b):
            samples = jnp.concatenate(
                [recv[k, pl.ds(first, per_chunk)].reshape(per_chunk * block, block) for k in range(8)], axis=1
            )
            spectra = matmul_nt(table[b, 0], samples) + matmul_nt(table[b, 1], samples)
            for m in range(per_chunk):
                rows = pl.ds(b * (FBLOCK * members) + first + m, FBLOCK, stride=members)
                columns = slice(m * block, (m + 1) * block)
                xre[rows, :] = spectra[:FBLOCK, columns]
                xim[rows, :] = spectra[FBLOCK:, columns]

    lane = lax.broadcasted_iota(jnp.int32, (members, 4 * members), 1)
    row = lax.broadcasted_iota(jnp.int32, (members, 4 * members), 0)
    lane_f, lane_j = lane // members, lane % members
    half = members // 2

    def pick(tile):
        out = tile[3 * members :]
        for f in range(3):
            out = jnp.where(lane_f == f, tile[f * members : (f + 1) * members], out)
        return out

    def cross(zz, yy, t, cc):
        width = 4 * members
        rows = pl.ds((zz * 32 + yy * 16 + cc * 8 + t) * width, width)
        re_hi, re_lo = split(xre[rows, :])
        im_hi, im_lo = split(xim[rows, :])
        left = jnp.concatenate(
            [jnp.concatenate([re_hi, im_hi], axis=1), jnp.concatenate([re_lo, im_lo], axis=1)], axis=0
        )

        def right(re, im):
            re, im = re.T, im.T
            return jnp.concatenate(
                [jnp.concatenate([re, im], axis=0), jnp.concatenate([-im, re], axis=0)], axis=1
            )

        both = matmul(left, right(re_hi, im_hi))
        gram = both[:width] + both[width:] + matmul(left[:width], right(re_lo, im_lo))
        return jnp.where(row >= lane_j, pick(gram[:, :width]), pick(gram[:, width:]))

    def to_core(n):
        zz = (z + 1 + n) % 4
        return pltpu.make_async_remote_copy(
            src_ref=part.at[0, zz],
            dst_ref=got_core.at[zz],
            send_sem=core_send.at[n],
            recv_sem=core_recv.at[n],
            device_id=(space + 1 - 2 * core, tm),
            device_id_type=MESH,
        )

    def over_z(stage, d):
        zz = (z + d) % 4
        src, dst = ((part.at[1, zz, 0], got_z.at[d]), (part.at[1, zz, 1, plane], got_pz.at[d]))[stage]
        return pltpu.make_async_remote_copy(
            src_ref=src,
            dst_ref=dst,
            send_sem=z_send.at[stage, d],
            recv_sem=z_recv.at[stage, d],
            device_id=device(zz, plane, core),
            device_id_type=MESH,
        )

    def over_plane(n, d):
        pp, zz = plane_peer(d), (z + 1 + n) % 4
        src, dst = (part.at[1, zz, 1, pp], got_p.at[zz, d])
        if isinstance(n, int) and n == 4:
            src, dst = part.at[1, z, 0, pp], got_zp.at[d]
        return pltpu.make_async_remote_copy(
            src_ref=src,
            dst_ref=dst,
            send_sem=p_send.at[n, d],
            recv_sem=p_recv.at[n, d],
            device_id=device(z, pp, core),
            device_id_type=MESH,
        )

    @pl.loop(0, 4)
    def _(n):
        zz = (z + 1 + n) % 4

        for pp in range(16):
            tile = cross(zz, pp // 8, pp % 8, 1 - core)
            part[0, zz, 0, pp] = tile[:half]
            part[0, zz, 1, pp] = tile[half:]

        to_core(n).start()

    @pl.loop(0, 4)
    def _(n):
        zz = (z + 1 + n) % 4
        to_core(n).wait_recv()

        for pp in range(16):
            tile = cross(zz, pp // 8, pp % 8, core)
            part[1, zz, 0, pp] = tile[:half] + got_core[zz, 0, pp]
            part[1, zz, 1, pp] = tile[half:] + got_core[zz, 1, pp]

        @pl.when(n < 3)
        def _():
            over_z(0, n + 1).start()

        for d in range(1, 16):
            over_plane(n, d).start()

    def lower_sum(n):
        zz = (z + 1 + n) % 4
        for d in range(1, 16):
            over_plane(n, d).wait_recv()
        total = part[1, zz, 1, plane]
        for d in range(1, 16):
            total = total + got_p[zz, d]
        return total

    for n in range(3):
        part[1, (z + 1 + n) % 4, 1, plane] = lower_sum(n)
        over_z(1, n + 1).start()
    for d in range(1, 4):
        over_z(0, d).wait_recv()
    part[1, z, 0] += got_z[1] + got_z[2] + got_z[3]
    for d in range(1, 16):
        over_plane(4, d).start()
    lower = lower_sum(3)
    for d in range(1, 4):
        over_z(1, d).wait_recv()
        lower = lower + got_pz[d]
    upper = part[1, z, 0, plane]
    for d in range(1, 16):
        over_plane(4, d).wait_recv()
        upper = upper + got_zp[d]

    mixed = jnp.concatenate([upper, lower], axis=0) * norm
    spread = jnp.concatenate([jnp.where(lane_f == f, mixed, 0.0) for f in range(4)], axis=0).T
    turned = spread[:members]
    for f in range(1, 4):
        turned = turned + spread[f * members : (f + 1) * members]
    real = jnp.where(row >= lane_j, mixed, turned)
    imag = jnp.where(row < lane_j, mixed, jnp.where(row == lane_j, 0.0, -turned))
    for which, value in enumerate((real, imag)):
        for bit in (2, 1):
            row_bit, lane_bit = row // bit % 2, lane_f // bit % 2
            up = pltpu.roll(pltpu.roll(value, bit * members, 1), members - bit, 0)
            down = pltpu.roll(pltpu.roll(value, (4 - bit) * members, 1), bit, 0)
            value = jnp.where(row_bit == lane_bit, value, jnp.where(row_bit == 0, up, down))
        for u in range(members // 4):
            start = (which * members // 4 + u) * 4 * members
            o_ref[:, start : start + 4 * members] = value[4 * u : 4 * u + 4]

    @pl.loop(0, CHUNKS)
    def _(c):
        for r in range(len(TM_PEERS)):
            snapshots(c, r).wait_send()

    for n in range(4):
        to_core(n).wait_send()
    for d in range(1, 4):
        over_z(0, d).wait_send()
        over_z(1, d).wait_send()
    for n in range(5):
        for d in range(1, 16):
            over_plane(n, d).wait_send()


def shards(series):
    members, pts_dev, frames_dev = series.shape
    space_count, time_count = lax.axis_size("space"), lax.axis_size("tm")
    frames, block = frames_dev * time_count, pts_dev // time_count
    nfreq, half = frames // 2, members // 2
    norm = 1.0 / (0.375 * frames * pts_dev * space_count)
    table = dft_table(frames)
    f32, bf16 = jnp.float32, jnp.bfloat16
    width = 4 * members
    dma = pltpu.SemaphoreType.DMA
    return pl.pallas_call(
        functools.partial(kernel, norm),
        out_shape=jax.ShapeDtypeStruct((nfreq // (space_count * time_count), 2 * members * members), f32),
        in_specs=[pl.BlockSpec(memory_space=pl.ANY)] * 2,
        out_specs=pl.BlockSpec(memory_space=pltpu.VMEM),
        scratch_shapes=[
            pltpu.VMEM((time_count, members, block, frames_dev), bf16),
            pltpu.VMEM(table.shape, bf16),
            pltpu.VMEM((nfreq * members, block), f32),
            pltpu.VMEM((nfreq * members, block), f32),
            pltpu.VMEM((2, 4, 2, 16, half, width), f32),
            pltpu.VMEM((4, 2, 16, half, width), f32),
            pltpu.VMEM((4, 16, half, width), f32),
            pltpu.VMEM((16, half, width), f32),
            pltpu.VMEM((4, 16, half, width), f32),
            pltpu.VMEM((4, half, width), f32),
            dma, dma, dma((CHUNKS, 7)), dma((CHUNKS, 7)), dma((4,)), dma((4,)),
            dma((2, 4)), dma((2, 4)), dma((5, 16)), dma((5, 16)),
        ],
        compiler_params=pltpu.CompilerParams(collective_id=0, has_side_effects=True, vmem_limit_bytes=56 << 20),
    )(series, jnp.asarray(table))


def solution(mesh):
    placed = (P(None, "space", "tm"),)
    return jax.shard_map(
        shards, mesh=mesh, in_specs=placed, out_specs=P(("space", "tm"), None), check_vma=False
    )
```

```python
import functools
import math

import jax
import jax.numpy as jnp
import ml_dtypes
import numpy as np
from jax import lax
from jax.experimental import pallas as pl
from jax.experimental.pallas import tpu as pltpu
from jax.sharding import PartitionSpec as P

MESH = pl.DeviceIdType.MESH
NT_DIMS = (((1,), (1,)), ((), ()))
CHUNKS = 16
GROUPS = 2
FBLOCK = 128
TM_PEERS = ((1, 0), (2, 1), (3, 0), (0, 1), (1, 1), (2, 0), (3, 1))


def dft_table(frames):
    nfreq = frames // 2
    t = np.arange(frames)
    angle = 2.0 * np.pi * (np.arange(nfreq)[:, None] * t[None, :] % frames) / frames
    window = 0.5 - 0.5 * np.cos(2.0 * np.pi * t / frames)
    table = np.stack([np.cos(angle), -np.sin(angle)]) * window
    table = table - table.sum(axis=2, keepdims=True) / frames
    table[np.abs(table) < 1e-13] = 0.0
    bf16 = ml_dtypes.bfloat16
    high = table.astype(np.float32).astype(bf16)
    low = (table - high.astype(np.float64)).astype(np.float32).astype(bf16)
    high = high.reshape(2 * nfreq, frames)
    low = low.reshape(2 * nfreq, frames)
    order = np.argsort(np.abs(low.astype(np.float64)), axis=1)
    for first, count in ((0, 32), (32, 4), (36, 1), (37, 1)):
        rest = (high.astype(np.float64) + low.astype(np.float64)).sum(axis=1, keepdims=True)
        cols = order[:, first : first + count]
        rows = np.arange(2 * nfreq)[:, None]
        low[rows, cols] = (low[rows, cols].astype(np.float64) - rest / count).astype(np.float32).astype(bf16)
    parts = np.stack([high, low]).reshape(2, 2, nfreq // FBLOCK, FBLOCK, frames)
    return parts.transpose(2, 0, 1, 3, 4).reshape(nfreq // FBLOCK, 2, 2 * FBLOCK, frames)


def split(value):
    high = value.astype(jnp.bfloat16)
    return high, (value - high.astype(jnp.float32)).astype(jnp.bfloat16)


def matmul_nt(a, b):
    return lax.dot_general(a, b, NT_DIMS, preferred_element_type=jnp.float32)


def matmul(a, b):
    return jnp.dot(a, b, preferred_element_type=jnp.float32)


def kernel(
    norm, x_ref, table_ref, o_ref,
    recv, table, xre, xim, part, got_core, got_z, got_zp, got_p, got_pz,
    local_sem, table_sem, a2a_send, a2a_recv, core_send, core_recv, z_send, z_recv, p_send, p_recv,
):
    space, tm = lax.axis_index("space"), lax.axis_index("tm")
    core, y_hi, z = space % 2, space // 2 % 2, space // 4
    x, y_lo = tm % 4, tm // 4
    members, block = recv.shape[1], recv.shape[2]
    per_chunk = members // CHUNKS
    nfreq = xre.shape[0] // members
    plane = y_hi * 8 + y_lo * 4 + x

    def tm_peer(r):
        dx, dy = TM_PEERS[r]
        return (y_lo + dy) % 2 * 4 + (x + dx) % 4

    def tm_source(r):
        dx, dy = TM_PEERS[r]
        return (y_lo + 2 - dy) % 2 * 4 + (x + 4 - dx) % 4

    def device(z, plane, core):
        return z * 4 + plane // 8 * 2 + core, plane % 8

    def plane_peer(d):
        dyh, dyl, dx = d // 8, d // 4 % 2, d % 4
        ahead = (y_hi + dyh) % 2 * 8 + (y_lo + dyl) % 2 * 4 + (x + dx) % 4
        return ahead

    barrier = pltpu.get_barrier_semaphore()
    greeted = [device(z, plane_peer(d), core) for d in range(1, 16)]
    greeted += [device((z + d) % 4, plane, core) for d in range(1, 4)]
    greeted += [device(z, plane, 1 - core)]
    for peer in greeted:
        pl.semaphore_signal(barrier, inc=1, device_id=peer, device_id_type=MESH)
    pl.semaphore_wait(barrier, len(greeted))

    def snapshots(c, r):
        peer = tm_peer(r)
        return pltpu.make_async_remote_copy(
            src_ref=x_ref.at[pl.ds(c * per_chunk, per_chunk), pl.ds(peer * block, block), :],
            dst_ref=recv.at[tm, pl.ds(c * per_chunk, per_chunk)],
            send_sem=a2a_send.at[c, r],
            recv_sem=a2a_recv.at[c, r],
            device_id=(space, peer),
            device_id_type=MESH,
        )

    @pl.loop(0, CHUNKS)
    def _(c):
        for r in range(len(TM_PEERS)):
            snapshots(c, r).start()

    table_copy = pltpu.make_async_copy(table_ref, table, table_sem)
    table_copy.start()
    own_copy = pltpu.make_async_copy(x_ref.at[:, pl.ds(tm * block, block), :], recv.at[tm], local_sem)
    own_copy.start()
    table_copy.wait()
    own_copy.wait()

    @pl.loop(0, CHUNKS)
    def _(c):
        for r in range(len(TM_PEERS)):
            snapshots(c, r).wait_recv()
        first = c * per_chunk

        @pl.loop(0, nfreq // FBLOCK)
        def _(b):
            samples = jnp.concatenate(
                [recv[k, pl.ds(first, per_chunk)].reshape(per_chunk * block, block) for k in range(8)], axis=1
            )
            spectra = matmul_nt(table[b, 0], samples) + matmul_nt(table[b, 1], samples)
            for m in range(per_chunk):
                rows = pl.ds(b * (FBLOCK * members) + first + m, FBLOCK, stride=members)
                columns = slice(m * block, (m + 1) * block)
                xre[rows, :] = spectra[:FBLOCK, columns]
                xim[rows, :] = spectra[FBLOCK:, columns]

    lane = lax.broadcasted_iota(jnp.int32, (members, 4 * members), 1)
    row = lax.broadcasted_iota(jnp.int32, (members, 4 * members), 0)
    lane_f, lane_j = lane // members, lane % members
    half = members // 2

    def pick(tile):
        out = tile[3 * members :]
        for f in range(3):
            out = jnp.where(lane_f == f, tile[f * members : (f + 1) * members], out)
        return out

    def cross(zz, yy, t, cc):
        width = 4 * members
        rows = pl.ds((zz * 32 + yy * 16 + cc * 8 + t) * width, width)
        re_hi, re_lo = split(xre[rows, :])
        im_hi, im_lo = split(xim[rows, :])
        left = jnp.concatenate(
            [jnp.concatenate([re_hi, im_hi], axis=1), jnp.concatenate([re_lo, im_lo], axis=1)], axis=0
        )

        def right(re, im):
            re, im = re.T, im.T
            return jnp.concatenate(
                [jnp.concatenate([re, im], axis=0), jnp.concatenate([-im, re], axis=0)], axis=1
            )

        both = matmul(left, right(re_hi, im_hi))
        gram = both[:width] + both[width:] + matmul(left[:width], right(re_lo, im_lo))
        return jnp.where(row >= lane_j, pick(gram[:, :width]), pick(gram[:, width:]))

    def to_core(n):
        return pltpu.make_async_remote_copy(
            src_ref=part.at[0, n],
            dst_ref=got_core.at[n],
            send_sem=core_send.at[n],
            recv_sem=core_recv.at[n],
            device_id=(space + 1 - 2 * core, tm),
            device_id_type=MESH,
        )

    def over_z(stage, d):
        zz = (z + d) % 4
        src, dst = ((part.at[1, d - 1, 0], got_z.at[d]), (part.at[1, d - 1, 1, plane], got_pz.at[d]))[stage]
        return pltpu.make_async_remote_copy(
            src_ref=src,
            dst_ref=dst,
            send_sem=z_send.at[stage, d],
            recv_sem=z_recv.at[stage, d],
            device_id=device(zz, plane, core),
            device_id_type=MESH,
        )

    def over_plane(k, d):
        pp = plane_peer(d)
        if isinstance(k, int) and k == GROUPS:
            src, dst = part.at[1, 3, 0, pp], got_zp.at[d]
        else:
            some = pl.ds(k * (4 // GROUPS), 4 // GROUPS)
            src, dst = part.at[1, some, 1, pp], got_p.at[some, d]
        return pltpu.make_async_remote_copy(
            src_ref=src,
            dst_ref=dst,
            send_sem=p_send.at[k, d],
            recv_sem=p_recv.at[k, d],
            device_id=device(z, pp, core),
            device_id_type=MESH,
        )

    @pl.loop(0, 5)
    def _(step):
        @pl.when(step < 4)
        def _():
            zz = (z + 1 + step) % 4
            for pp in range(16):
                tile = cross(zz, pp // 8, pp % 8, 1 - core)
                part[0, step, 0, pp] = tile[:half]
                part[0, step, 1, pp] = tile[half:]
            to_core(step).start()

        @pl.when(step > 0)
        def _():
            n = step - 1
            zz = (z + 1 + n) % 4
            to_core(n).wait_recv()
            for pp in range(16):
                tile = cross(zz, pp // 8, pp % 8, core)
                part[1, n, 0, pp] = tile[:half] + got_core[n, 0, pp]
                part[1, n, 1, pp] = tile[half:] + got_core[n, 1, pp]

            @pl.when(n < 3)
            def _():
                over_z(0, n + 1).start()

            @pl.when(step % (4 // GROUPS) == 0)
            def _():
                for d in range(1, 16):
                    over_plane(n // (4 // GROUPS), d).start()

    def lower_sum(n):
        if n % (4 // GROUPS) == 0:
            for d in range(1, 16):
                over_plane(n // (4 // GROUPS), d).wait_recv()
        total = part[1, n, 1, plane]
        for d in range(1, 16):
            total = total + got_p[n, d]
        return total

    for n in range(3):
        part[1, n, 1, plane] = lower_sum(n)
        over_z(1, n + 1).start()
    for d in range(1, 4):
        over_z(0, d).wait_recv()
    part[1, 3, 0] += got_z[1] + got_z[2] + got_z[3]
    for d in range(1, 16):
        over_plane(GROUPS, d).start()
    lower = lower_sum(3)
    for d in range(1, 4):
        over_z(1, d).wait_recv()
        lower = lower + got_pz[d]
    upper = part[1, 3, 0, plane]
    for d in range(1, 16):
        over_plane(GROUPS, d).wait_recv()
        upper = upper + got_zp[d]

    mixed = jnp.concatenate([upper, lower], axis=0) * norm
    spread = jnp.concatenate([jnp.where(lane_f == f, mixed, 0.0) for f in range(4)], axis=0).T
    turned = spread[:members]
    for f in range(1, 4):
        turned = turned + spread[f * members : (f + 1) * members]
    real = jnp.where(row >= lane_j, mixed, turned)
    imag = jnp.where(row < lane_j, mixed, jnp.where(row == lane_j, 0.0, -turned))
    for which, value in enumerate((real, imag)):
        for bit in (2, 1):
            row_bit, lane_bit = row // bit % 2, lane_f // bit % 2
            up = pltpu.roll(pltpu.roll(value, bit * members, 1), members - bit, 0)
            down = pltpu.roll(pltpu.roll(value, (4 - bit) * members, 1), bit, 0)
            value = jnp.where(row_bit == lane_bit, value, jnp.where(row_bit == 0, up, down))
        for u in range(members // 4):
            start = (which * members // 4 + u) * 4 * members
            o_ref[:, start : start + 4 * members] = value[4 * u : 4 * u + 4]

    @pl.loop(0, CHUNKS)
    def _(c):
        for r in range(len(TM_PEERS)):
            snapshots(c, r).wait_send()

    for n in range(4):
        to_core(n).wait_send()
    for d in range(1, 4):
        over_z(0, d).wait_send()
        over_z(1, d).wait_send()
    for k in range(GROUPS + 1):
        for d in range(1, 16):
            over_plane(k, d).wait_send()


def shards(series):
    members, pts_dev, frames_dev = series.shape
    space_count, time_count = lax.axis_size("space"), lax.axis_size("tm")
    frames, block = frames_dev * time_count, pts_dev // time_count
    nfreq, half = frames // 2, members // 2
    norm = 1.0 / (0.375 * frames * pts_dev * space_count)
    table = dft_table(frames)
    f32, bf16 = jnp.float32, jnp.bfloat16
    width = 4 * members
    dma = pltpu.SemaphoreType.DMA
    return pl.pallas_call(
        functools.partial(kernel, norm),
        out_shape=jax.ShapeDtypeStruct((nfreq // (space_count * time_count), 2 * members * members), f32),
        in_specs=[pl.BlockSpec(memory_space=pl.ANY)] * 2,
        out_specs=pl.BlockSpec(memory_space=pltpu.VMEM),
        scratch_shapes=[
            pltpu.VMEM((time_count, members, block, frames_dev), bf16),
            pltpu.VMEM(table.shape, bf16),
            pltpu.VMEM((nfreq * members, block), f32),
            pltpu.VMEM((nfreq * members, block), f32),
            pltpu.VMEM((2, 4, 2, 16, half, width), f32),
            pltpu.VMEM((4, 2, 16, half, width), f32),
            pltpu.VMEM((4, 16, half, width), f32),
            pltpu.VMEM((16, half, width), f32),
            pltpu.VMEM((4, 16, half, width), f32),
            pltpu.VMEM((4, half, width), f32),
            dma, dma, dma((CHUNKS, 7)), dma((CHUNKS, 7)), dma((4,)), dma((4,)),
            dma((2, 4)), dma((2, 4)), dma((GROUPS + 1, 16)), dma((GROUPS + 1, 16)),
        ],
        compiler_params=pltpu.CompilerParams(collective_id=0, has_side_effects=True, vmem_limit_bytes=56 << 20),
    )(series, jnp.asarray(table))


def solution(mesh):
    placed = (P(None, "space", "tm"),)
    return jax.shard_map(
        shards, mesh=mesh, in_specs=placed, out_specs=P(("space", "tm"), None), check_vma=False
    )
```

```python
import functools
import math

import jax
import jax.numpy as jnp
import ml_dtypes
import numpy as np
from jax import lax
from jax.experimental import pallas as pl
from jax.experimental.pallas import tpu as pltpu
from jax.sharding import PartitionSpec as P

MESH = pl.DeviceIdType.MESH
NT_DIMS = (((1,), (1,)), ((), ()))
CHUNKS = 16
GROUPS = 2
FBLOCK = 128
TM_PEERS = ((1, 0), (2, 1), (3, 0), (0, 1), (1, 1), (2, 0), (3, 1))


def dft_table(frames):
    nfreq = frames // 2
    t = np.arange(frames)
    angle = 2.0 * np.pi * (np.arange(nfreq)[:, None] * t[None, :] % frames) / frames
    window = 0.5 - 0.5 * np.cos(2.0 * np.pi * t / frames)
    table = np.stack([np.cos(angle), -np.sin(angle)]) * window
    table = table - table.sum(axis=2, keepdims=True) / frames
    table[np.abs(table) < 1e-13] = 0.0
    bf16 = ml_dtypes.bfloat16
    high = table.astype(np.float32).astype(bf16)
    low = (table - high.astype(np.float64)).astype(np.float32).astype(bf16)
    high = high.reshape(2 * nfreq, frames)
    low = low.reshape(2 * nfreq, frames)
    order = np.argsort(np.abs(low.astype(np.float64)), axis=1)
    for first, count in ((0, 32), (32, 4), (36, 1), (37, 1)):
        rest = (high.astype(np.float64) + low.astype(np.float64)).sum(axis=1, keepdims=True)
        cols = order[:, first : first + count]
        rows = np.arange(2 * nfreq)[:, None]
        low[rows, cols] = (low[rows, cols].astype(np.float64) - rest / count).astype(np.float32).astype(bf16)
    parts = np.stack([high, low]).reshape(2, 2, nfreq // FBLOCK, FBLOCK, frames)
    return parts.transpose(2, 0, 1, 3, 4).reshape(nfreq // FBLOCK, 2, 2 * FBLOCK, frames)


def split(value):
    high = value.astype(jnp.bfloat16)
    return high, (value - high.astype(jnp.float32)).astype(jnp.bfloat16)


def matmul_nt(a, b):
    return lax.dot_general(a, b, NT_DIMS, preferred_element_type=jnp.float32)


def matmul(a, b):
    return jnp.dot(a, b, preferred_element_type=jnp.float32)


def kernel(
    norm, x_ref, table_ref, o_ref,
    recv, table, xre, xim, part, got_core, got_z, got_zp, got_p, got_pz,
    local_sem, table_sem, a2a_send, a2a_recv, core_send, core_recv, z_send, z_recv, p_send, p_recv,
):
    space, tm = lax.axis_index("space"), lax.axis_index("tm")
    core, y_hi, z = space % 2, space // 2 % 2, space // 4
    x, y_lo = tm % 4, tm // 4
    members, block = recv.shape[1], recv.shape[2]
    per_chunk = members // CHUNKS
    nfreq = xre.shape[0] // members
    plane = y_hi * 8 + y_lo * 4 + x

    def tm_peer(r):
        dx, dy = TM_PEERS[r]
        return (y_lo + dy) % 2 * 4 + (x + dx) % 4

    def tm_source(r):
        dx, dy = TM_PEERS[r]
        return (y_lo + 2 - dy) % 2 * 4 + (x + 4 - dx) % 4

    def device(z, plane, core):
        return z * 4 + plane // 8 * 2 + core, plane % 8

    def plane_peer(d):
        dyh, dyl, dx = d // 8, d // 4 % 2, d % 4
        ahead = (y_hi + dyh) % 2 * 8 + (y_lo + dyl) % 2 * 4 + (x + dx) % 4
        return ahead

    barrier = pltpu.get_barrier_semaphore()
    greeted = [device(z, plane_peer(d), core) for d in range(1, 16)]
    greeted += [device((z + d) % 4, plane, core) for d in range(1, 4)]
    greeted += [device(z, plane, 1 - core)]
    for peer in greeted:
        pl.semaphore_signal(barrier, inc=1, device_id=peer, device_id_type=MESH)
    pl.semaphore_wait(barrier, len(greeted))

    def snapshots(c, r):
        peer = tm_peer(r)
        return pltpu.make_async_remote_copy(
            src_ref=x_ref.at[pl.ds(c * per_chunk, per_chunk), pl.ds(peer * block, block), :],
            dst_ref=recv.at[tm, pl.ds(c * per_chunk, per_chunk)],
            send_sem=a2a_send.at[c, r],
            recv_sem=a2a_recv.at[c, r],
            device_id=(space, peer),
            device_id_type=MESH,
        )

    @pl.loop(0, CHUNKS)
    def _(c):
        for r in range(len(TM_PEERS)):
            snapshots(c, r).start()

    table_copy = pltpu.make_async_copy(table_ref, table, table_sem)
    table_copy.start()
    own_copy = pltpu.make_async_copy(x_ref.at[:, pl.ds(tm * block, block), :], recv.at[tm], local_sem)
    own_copy.start()
    table_copy.wait()
    own_copy.wait()

    @pl.loop(0, CHUNKS)
    def _(c):
        for r in range(len(TM_PEERS)):
            snapshots(c, r).wait_recv()
        first = c * per_chunk

        @pl.loop(0, nfreq // FBLOCK)
        def _(b):
            samples = jnp.concatenate(
                [recv[k, pl.ds(first, per_chunk)].reshape(per_chunk * block, block) for k in range(8)], axis=1
            )
            spectra = matmul_nt(table[b, 0], samples) + matmul_nt(table[b, 1], samples)
            for m in range(per_chunk):
                rows = pl.ds(b * (FBLOCK * members) + first + m, FBLOCK, stride=members)
                columns = slice(m * block, (m + 1) * block)
                xre[rows, :] = spectra[:FBLOCK, columns]
                xim[rows, :] = spectra[FBLOCK:, columns]

    lane = lax.broadcasted_iota(jnp.int32, (members, 4 * members), 1)
    row = lax.broadcasted_iota(jnp.int32, (members, 4 * members), 0)
    lane_f, lane_j = lane // members, lane % members
    half = members // 2

    def pick(tile):
        out = tile[3 * members :]
        for f in range(3):
            out = jnp.where(lane_f == f, tile[f * members : (f + 1) * members], out)
        return out

    def cross(zz, yy, t, cc):
        width = 4 * members
        rows = pl.ds((zz * 32 + yy * 16 + cc * 8 + t) * width, width)
        re_hi, re_lo = split(xre[rows, :])
        im_hi, im_lo = split(xim[rows, :])
        left = jnp.concatenate(
            [jnp.concatenate([re_hi, im_hi], axis=1), jnp.concatenate([re_lo, im_lo], axis=1)], axis=0
        )

        def right(re, im):
            re, im = re.T, im.T
            return jnp.concatenate(
                [jnp.concatenate([re, im], axis=0), jnp.concatenate([-im, re], axis=0)], axis=1
            )

        both = matmul(left, right(re_hi, im_hi))
        gram = both[:width] + both[width:] + matmul(left[:width], right(re_lo, im_lo))
        return jnp.where(row >= lane_j, pick(gram[:, :width]), pick(gram[:, width:]))

    def to_core(n):
        return pltpu.make_async_remote_copy(
            src_ref=part.at[0, n],
            dst_ref=got_core.at[n],
            send_sem=core_send.at[n],
            recv_sem=core_recv.at[n],
            device_id=(space + 1 - 2 * core, tm),
            device_id_type=MESH,
        )

    def over_z(stage, d):
        zz = (z + d) % 4
        src, dst = ((part.at[1, d - 1, 0], got_z.at[d]), (part.at[1, d - 1, 1, plane], got_pz.at[d]))[stage]
        return pltpu.make_async_remote_copy(
            src_ref=src,
            dst_ref=dst,
            send_sem=z_send.at[stage, d],
            recv_sem=z_recv.at[stage, d],
            device_id=device(zz, plane, core),
            device_id_type=MESH,
        )

    def over_plane(k, d):
        pp = plane_peer(d)
        if isinstance(k, int) and k == GROUPS:
            src, dst = part.at[1, 3, 0, pp], got_zp.at[d]
        else:
            some = pl.ds(k * (4 // GROUPS), 4 // GROUPS)
            src, dst = part.at[1, some, 1, pp], got_p.at[some, d]
        return pltpu.make_async_remote_copy(
            src_ref=src,
            dst_ref=dst,
            send_sem=p_send.at[k, d],
            recv_sem=p_recv.at[k, d],
            device_id=device(z, pp, core),
            device_id_type=MESH,
        )

    @pl.loop(0, 5)
    def _(step):
        @pl.when(step < 4)
        def _():
            zz = (z + 1 + step) % 4
            for pp in range(16):
                tile = cross(zz, pp // 8, pp % 8, 1 - core)
                part[0, step, 0, pp] = tile[:half]
                part[0, step, 1, pp] = tile[half:]
            to_core(step).start()

        @pl.when(step > 0)
        def _():
            n = step - 1
            zz = (z + 1 + n) % 4
            to_core(n).wait_recv()
            for pp in range(16):
                tile = cross(zz, pp // 8, pp % 8, core)
                part[1, n, 0, pp] = tile[:half] + got_core[n, 0, pp]
                part[1, n, 1, pp] = tile[half:] + got_core[n, 1, pp]

            @pl.when(n < 3)
            def _():
                over_z(0, n + 1).start()

            @pl.when(step % (4 // GROUPS) == 0)
            def _():
                for d in range(1, 16):
                    over_plane(n // (4 // GROUPS), d).start()

    def lower_sum(n):
        if n % (4 // GROUPS) == 0:
            for d in range(1, 16):
                over_plane(n // (4 // GROUPS), d).wait_recv()
        total = part[1, n, 1, plane]
        for d in range(1, 16):
            total = total + got_p[n, d]
        return total

    def pass_lower(n):
        part[1, n, 1, plane] = lower_sum(n)
        over_z(1, n + 1).start()

    for n in range(2):
        pass_lower(n)
    for d in range(1, 4):
        over_z(0, d).wait_recv()
    part[1, 3, 0] += got_z[1] + got_z[2] + got_z[3]
    for d in range(1, 16):
        over_plane(GROUPS, d).start()
    pass_lower(2)
    lower = lower_sum(3)
    for d in range(1, 4):
        over_z(1, d).wait_recv()
        lower = lower + got_pz[d]
    upper = part[1, 3, 0, plane]
    for d in range(1, 16):
        over_plane(GROUPS, d).wait_recv()
        upper = upper + got_zp[d]

    mixed = jnp.concatenate([upper, lower], axis=0) * norm
    spread = jnp.concatenate([jnp.where(lane_f == f, mixed, 0.0) for f in range(4)], axis=0).T
    turned = spread[:members]
    for f in range(1, 4):
        turned = turned + spread[f * members : (f + 1) * members]
    real = jnp.where(row >= lane_j, mixed, turned)
    imag = jnp.where(row < lane_j, mixed, jnp.where(row == lane_j, 0.0, -turned))
    for which, value in enumerate((real, imag)):
        for bit in (2, 1):
            row_bit, lane_bit = row // bit % 2, lane_f // bit % 2
            up = pltpu.roll(pltpu.roll(value, bit * members, 1), members - bit, 0)
            down = pltpu.roll(pltpu.roll(value, (4 - bit) * members, 1), bit, 0)
            value = jnp.where(row_bit == lane_bit, value, jnp.where(row_bit == 0, up, down))
        for u in range(members // 4):
            start = (which * members // 4 + u) * 4 * members
            o_ref[:, start : start + 4 * members] = value[4 * u : 4 * u + 4]

    @pl.loop(0, CHUNKS)
    def _(c):
        for r in range(len(TM_PEERS)):
            snapshots(c, r).wait_send()

    for n in range(4):
        to_core(n).wait_send()
    for d in range(1, 4):
        over_z(0, d).wait_send()
        over_z(1, d).wait_send()
    for k in range(GROUPS + 1):
        for d in range(1, 16):
            over_plane(k, d).wait_send()


def shards(series):
    members, pts_dev, frames_dev = series.shape
    space_count, time_count = lax.axis_size("space"), lax.axis_size("tm")
    frames, block = frames_dev * time_count, pts_dev // time_count
    nfreq, half = frames // 2, members // 2
    norm = 1.0 / (0.375 * frames * pts_dev * space_count)
    table = dft_table(frames)
    f32, bf16 = jnp.float32, jnp.bfloat16
    width = 4 * members
    dma = pltpu.SemaphoreType.DMA
    return pl.pallas_call(
        functools.partial(kernel, norm),
        out_shape=jax.ShapeDtypeStruct((nfreq // (space_count * time_count), 2 * members * members), f32),
        in_specs=[pl.BlockSpec(memory_space=pl.ANY)] * 2,
        out_specs=pl.BlockSpec(memory_space=pltpu.VMEM),
        scratch_shapes=[
            pltpu.VMEM((time_count, members, block, frames_dev), bf16),
            pltpu.VMEM(table.shape, bf16),
            pltpu.VMEM((nfreq * members, block), f32),
            pltpu.VMEM((nfreq * members, block), f32),
            pltpu.VMEM((2, 4, 2, 16, half, width), f32),
            pltpu.VMEM((4, 2, 16, half, width), f32),
            pltpu.VMEM((4, 16, half, width), f32),
            pltpu.VMEM((16, half, width), f32),
            pltpu.VMEM((4, 16, half, width), f32),
            pltpu.VMEM((4, half, width), f32),
            dma, dma, dma((CHUNKS, 7)), dma((CHUNKS, 7)), dma((4,)), dma((4,)),
            dma((2, 4)), dma((2, 4)), dma((GROUPS + 1, 16)), dma((GROUPS + 1, 16)),
        ],
        compiler_params=pltpu.CompilerParams(collective_id=0, has_side_effects=True, vmem_limit_bytes=56 << 20),
    )(series, jnp.asarray(table))


def solution(mesh):
    placed = (P(None, "space", "tm"),)
    return jax.shard_map(
        shards, mesh=mesh, in_specs=placed, out_specs=P(("space", "tm"), None), check_vma=False
    )
```

```python
import functools
import math

import jax
import jax.numpy as jnp
import ml_dtypes
import numpy as np
from jax import lax
from jax.experimental import pallas as pl
from jax.experimental.pallas import tpu as pltpu
from jax.sharding import PartitionSpec as P

MESH = pl.DeviceIdType.MESH
NT_DIMS = (((1,), (1,)), ((), ()))
CHUNKS = 16
GROUPS = 4
FBLOCK = 128
TM_PEERS = ((1, 0), (2, 1), (3, 0), (0, 1), (1, 1), (2, 0), (3, 1))


def dft_table(frames):
    nfreq = frames // 2
    t = np.arange(frames)
    angle = 2.0 * np.pi * (np.arange(nfreq)[:, None] * t[None, :] % frames) / frames
    window = 0.5 - 0.5 * np.cos(2.0 * np.pi * t / frames)
    table = np.stack([np.cos(angle), -np.sin(angle)]) * window
    table = table - table.sum(axis=2, keepdims=True) / frames
    table[np.abs(table) < 1e-13] = 0.0
    bf16 = ml_dtypes.bfloat16
    high = table.astype(np.float32).astype(bf16)
    low = (table - high.astype(np.float64)).astype(np.float32).astype(bf16)
    high = high.reshape(2 * nfreq, frames)
    low = low.reshape(2 * nfreq, frames)
    order = np.argsort(np.abs(low.astype(np.float64)), axis=1)
    for first, count in ((0, 32), (32, 4), (36, 1), (37, 1)):
        rest = (high.astype(np.float64) + low.astype(np.float64)).sum(axis=1, keepdims=True)
        cols = order[:, first : first + count]
        rows = np.arange(2 * nfreq)[:, None]
        low[rows, cols] = (low[rows, cols].astype(np.float64) - rest / count).astype(np.float32).astype(bf16)
    parts = np.stack([high, low]).reshape(2, 2, nfreq // FBLOCK, FBLOCK, frames)
    return parts.transpose(2, 0, 1, 3, 4).reshape(nfreq // FBLOCK, 2, 2 * FBLOCK, frames)


def split(value):
    high = value.astype(jnp.bfloat16)
    return high, (value - high.astype(jnp.float32)).astype(jnp.bfloat16)


def matmul_nt(a, b):
    return lax.dot_general(a, b, NT_DIMS, preferred_element_type=jnp.float32)


def matmul(a, b):
    return jnp.dot(a, b, preferred_element_type=jnp.float32)


def kernel(
    norm, x_ref, table_ref, o_ref,
    recv, table, xre, xim, part, got_core, got_z, got_zp, got_p, got_pz,
    local_sem, table_sem, a2a_send, a2a_recv, core_send, core_recv, z_send, z_recv, p_send, p_recv,
):
    space, tm = lax.axis_index("space"), lax.axis_index("tm")
    core, y_hi, z = space % 2, space // 2 % 2, space // 4
    x, y_lo = tm % 4, tm // 4
    members, block = recv.shape[1], recv.shape[2]
    per_chunk = members // CHUNKS
    nfreq = xre.shape[0] // members
    plane = y_hi * 8 + y_lo * 4 + x

    def tm_peer(r):
        dx, dy = TM_PEERS[r]
        return (y_lo + dy) % 2 * 4 + (x + dx) % 4

    def tm_source(r):
        dx, dy = TM_PEERS[r]
        return (y_lo + 2 - dy) % 2 * 4 + (x + 4 - dx) % 4

    def device(z, plane, core):
        return z * 4 + plane // 8 * 2 + core, plane % 8

    def plane_peer(d):
        dyh, dyl, dx = d // 8, d // 4 % 2, d % 4
        ahead = (y_hi + dyh) % 2 * 8 + (y_lo + dyl) % 2 * 4 + (x + dx) % 4
        return ahead

    barrier = pltpu.get_barrier_semaphore()
    greeted = [device(z, plane_peer(d), core) for d in range(1, 16)]
    greeted += [device((z + d) % 4, plane, core) for d in range(1, 4)]
    greeted += [device(z, plane, 1 - core)]
    for peer in greeted:
        pl.semaphore_signal(barrier, inc=1, device_id=peer, device_id_type=MESH)
    pl.semaphore_wait(barrier, len(greeted))

    def snapshots(c, r):
        peer = tm_peer(r)
        return pltpu.make_async_remote_copy(
            src_ref=x_ref.at[pl.ds(c * per_chunk, per_chunk), pl.ds(peer * block, block), :],
            dst_ref=recv.at[tm, pl.ds(c * per_chunk, per_chunk)],
            send_sem=a2a_send.at[c, r],
            recv_sem=a2a_recv.at[c, r],
            device_id=(space, peer),
            device_id_type=MESH,
        )

    @pl.loop(0, CHUNKS)
    def _(c):
        for r in range(len(TM_PEERS)):
            snapshots(c, r).start()

    table_copy = pltpu.make_async_copy(table_ref, table, table_sem)
    table_copy.start()
    own_copy = pltpu.make_async_copy(x_ref.at[:, pl.ds(tm * block, block), :], recv.at[tm], local_sem)
    own_copy.start()
    table_copy.wait()
    own_copy.wait()

    @pl.loop(0, CHUNKS)
    def _(c):
        for r in range(len(TM_PEERS)):
            snapshots(c, r).wait_recv()
        first = c * per_chunk

        @pl.loop(0, nfreq // FBLOCK)
        def _(b):
            samples = jnp.concatenate(
                [recv[k, pl.ds(first, per_chunk)].reshape(per_chunk * block, block) for k in range(8)], axis=1
            )
            spectra = matmul_nt(table[b, 0], samples) + matmul_nt(table[b, 1], samples)
            for m in range(per_chunk):
                rows = pl.ds(b * (FBLOCK * members) + first + m, FBLOCK, stride=members)
                columns = slice(m * block, (m + 1) * block)
                xre[rows, :] = spectra[:FBLOCK, columns]
                xim[rows, :] = spectra[FBLOCK:, columns]

    lane = lax.broadcasted_iota(jnp.int32, (members, 4 * members), 1)
    row = lax.broadcasted_iota(jnp.int32, (members, 4 * members), 0)
    lane_f, lane_j = lane // members, lane % members
    half = members // 2

    def pick(tile):
        out = tile[3 * members :]
        for f in range(3):
            out = jnp.where(lane_f == f, tile[f * members : (f + 1) * members], out)
        return out

    def cross(zz, yy, t, cc):
        width = 4 * members
        rows = pl.ds((zz * 32 + yy * 16 + cc * 8 + t) * width, width)
        re_hi, re_lo = split(xre[rows, :])
        im_hi, im_lo = split(xim[rows, :])
        left = jnp.concatenate(
            [jnp.concatenate([re_hi, im_hi], axis=1), jnp.concatenate([re_lo, im_lo], axis=1)], axis=0
        )

        def right(re, im):
            re, im = re.T, im.T
            return jnp.concatenate(
                [jnp.concatenate([re, im], axis=0), jnp.concatenate([-im, re], axis=0)], axis=1
            )

        both = matmul(left, right(re_hi, im_hi))
        gram = both[:width] + both[width:] + matmul(left[:width], right(re_lo, im_lo))
        return jnp.where(row >= lane_j, pick(gram[:, :width]), pick(gram[:, width:]))

    def to_core(n):
        return pltpu.make_async_remote_copy(
            src_ref=part.at[0, n],
            dst_ref=got_core.at[n],
            send_sem=core_send.at[n],
            recv_sem=core_recv.at[n],
            device_id=(space + 1 - 2 * core, tm),
            device_id_type=MESH,
        )

    def over_z(stage, d):
        zz = (z + d) % 4
        src, dst = ((part.at[1, d - 1, 0], got_z.at[d]), (part.at[1, d - 1, 1, plane], got_pz.at[d]))[stage]
        return pltpu.make_async_remote_copy(
            src_ref=src,
            dst_ref=dst,
            send_sem=z_send.at[stage, d],
            recv_sem=z_recv.at[stage, d],
            device_id=device(zz, plane, core),
            device_id_type=MESH,
        )

    def over_plane(k, d):
        pp = plane_peer(d)
        if isinstance(k, int) and k == GROUPS:
            src, dst = part.at[1, 3, 0, pp], got_zp.at[d]
        else:
            some = pl.ds(k * (4 // GROUPS), 4 // GROUPS)
            src, dst = part.at[1, some, 1, pp], got_p.at[some, d]
        return pltpu.make_async_remote_copy(
            src_ref=src,
            dst_ref=dst,
            send_sem=p_send.at[k, d],
            recv_sem=p_recv.at[k, d],
            device_id=device(z, pp, core),
            device_id_type=MESH,
        )

    @pl.loop(0, 5)
    def _(step):
        @pl.when(step < 4)
        def _():
            zz = (z + 1 + step) % 4
            for pp in range(16):
                tile = cross(zz, pp // 8, pp % 8, 1 - core)
                part[0, step, 0, pp] = tile[:half]
                part[0, step, 1, pp] = tile[half:]
            to_core(step).start()

        @pl.when(step > 0)
        def _():
            n = step - 1
            zz = (z + 1 + n) % 4
            to_core(n).wait_recv()
            for pp in range(16):
                tile = cross(zz, pp // 8, pp % 8, core)
                part[1, n, 0, pp] = tile[:half] + got_core[n, 0, pp]
                part[1, n, 1, pp] = tile[half:] + got_core[n, 1, pp]

            @pl.when(n < 3)
            def _():
                over_z(0, n + 1).start()

            @pl.when(step % (4 // GROUPS) == 0)
            def _():
                for d in range(1, 16):
                    over_plane(n // (4 // GROUPS), d).start()

    def lower_sum(n):
        if n % (4 // GROUPS) == 0:
            for d in range(1, 16):
                over_plane(n // (4 // GROUPS), d).wait_recv()
        total = part[1, n, 1, plane]
        for d in range(1, 16):
            total = total + got_p[n, d]
        return total

    def pass_lower(n):
        part[1, n, 1, plane] = lower_sum(n)
        over_z(1, n + 1).start()

    for n in range(2):
        pass_lower(n)
    for d in range(1, 4):
        over_z(0, d).wait_recv()
    part[1, 3, 0] += got_z[1] + got_z[2] + got_z[3]
    for d in range(1, 16):
        over_plane(GROUPS, d).start()
    pass_lower(2)
    lower = lower_sum(3)
    for d in range(1, 4):
        over_z(1, d).wait_recv()
        lower = lower + got_pz[d]
    upper = part[1, 3, 0, plane]
    for d in range(1, 16):
        over_plane(GROUPS, d).wait_recv()
        upper = upper + got_zp[d]

    mixed = jnp.concatenate([upper, lower], axis=0) * norm
    spread = jnp.concatenate([jnp.where(lane_f == f, mixed, 0.0) for f in range(4)], axis=0).T
    turned = spread[:members]
    for f in range(1, 4):
        turned = turned + spread[f * members : (f + 1) * members]
    real = jnp.where(row >= lane_j, mixed, turned)
    imag = jnp.where(row < lane_j, mixed, jnp.where(row == lane_j, 0.0, -turned))
    for which, value in enumerate((real, imag)):
        for bit in (2, 1):
            row_bit, lane_bit = row // bit % 2, lane_f // bit % 2
            up = pltpu.roll(pltpu.roll(value, bit * members, 1), members - bit, 0)
            down = pltpu.roll(pltpu.roll(value, (4 - bit) * members, 1), bit, 0)
            value = jnp.where(row_bit == lane_bit, value, jnp.where(row_bit == 0, up, down))
        for u in range(members // 4):
            start = (which * members // 4 + u) * 4 * members
            o_ref[:, start : start + 4 * members] = value[4 * u : 4 * u + 4]

    @pl.loop(0, CHUNKS)
    def _(c):
        for r in range(len(TM_PEERS)):
            snapshots(c, r).wait_send()

    for n in range(4):
        to_core(n).wait_send()
    for d in range(1, 4):
        over_z(0, d).wait_send()
        over_z(1, d).wait_send()
    for k in range(GROUPS + 1):
        for d in range(1, 16):
            over_plane(k, d).wait_send()


def shards(series):
    members, pts_dev, frames_dev = series.shape
    space_count, time_count = lax.axis_size("space"), lax.axis_size("tm")
    frames, block = frames_dev * time_count, pts_dev // time_count
    nfreq, half = frames // 2, members // 2
    norm = 1.0 / (0.375 * frames * pts_dev * space_count)
    table = dft_table(frames)
    f32, bf16 = jnp.float32, jnp.bfloat16
    width = 4 * members
    dma = pltpu.SemaphoreType.DMA
    return pl.pallas_call(
        functools.partial(kernel, norm),
        out_shape=jax.ShapeDtypeStruct((nfreq // (space_count * time_count), 2 * members * members), f32),
        in_specs=[pl.BlockSpec(memory_space=pl.ANY)] * 2,
        out_specs=pl.BlockSpec(memory_space=pltpu.VMEM),
        scratch_shapes=[
            pltpu.VMEM((time_count, members, block, frames_dev), bf16),
            pltpu.VMEM(table.shape, bf16),
            pltpu.VMEM((nfreq * members, block), f32),
            pltpu.VMEM((nfreq * members, block), f32),
            pltpu.VMEM((2, 4, 2, 16, half, width), f32),
            pltpu.VMEM((4, 2, 16, half, width), f32),
            pltpu.VMEM((4, 16, half, width), f32),
            pltpu.VMEM((16, half, width), f32),
            pltpu.VMEM((4, 16, half, width), f32),
            pltpu.VMEM((4, half, width), f32),
            dma, dma, dma((CHUNKS, 7)), dma((CHUNKS, 7)), dma((4,)), dma((4,)),
            dma((2, 4)), dma((2, 4)), dma((GROUPS + 1, 16)), dma((GROUPS + 1, 16)),
        ],
        compiler_params=pltpu.CompilerParams(collective_id=0, has_side_effects=True, vmem_limit_bytes=56 << 20),
    )(series, jnp.asarray(table))


def solution(mesh):
    placed = (P(None, "space", "tm"),)
    return jax.shard_map(
        shards, mesh=mesh, in_specs=placed, out_specs=P(("space", "tm"), None), check_vma=False
    )
```
